32 devices in a mesh: samp: 2 (over core), grid: 16 (over z, y, x).
Axes of the slice: x: 2, y: 2, z: 4, core: 2. Of those that a mesh axis runs over, the one named last changes fastest.
Arguments:
- log_coef: float32 [2, 1024, 2048], P('samp', 'grid'), may hold values from -4 to 4
- source: float32 [2, 1024, 2048], P('samp', 'grid'), may hold values from -0.6 to 0.6
Outputs:
- correction: float32 [2, 1024, 2048], P('samp', 'grid')
- level_mean: float32 [1024, 2048], P('grid', 'samp')
- level_var: float32 [1024, 2048], P('grid', 'samp')
The draws below stay inside these ranges and needn't reach their ends.
All inputs are finite; a program needn't handle non-finite values.
Results may differ from the reference program's by a relative error of at most 0.0003.
Values sent between devices are 32-bit elements; how exact they have to be, the bound alone decides.
A program may use at most 192 MiB of HBM per device.

```python
import jax
import jax.numpy as jnp
from jax import lax

NY = 2048
LEVELS = 5
VCYCLES = 2
COARSE_SWEEPS = 4
NX = 1024
SAMPLES = 2


def level_of(stream_key, dims, shards, smallest, largest):
    factor_of, own = 1.0, jax.random.fold_in(stream_key, 6)
    for axis_at, parts in shards:
        heights = jnp.exp(jax.random.uniform(jax.random.fold_in(own, axis_at), (parts,), jnp.float32, smallest / len(shards), largest / len(shards)))
        factor_of = factor_of * jnp.repeat(heights, dims[axis_at] // parts).reshape([-1 if axis == axis_at else 1 for axis in range(len(dims))])
    return factor_of


def bell_draw(rng, extent, deviation, bound, pieces=(), held_as=jnp.bfloat16):
    loudness = level_of(rng, extent, pieces, -0.22, 0.18) if pieces else 1.0
    array = jax.random.normal(rng, extent, jnp.float32) * deviation * loudness
    return jnp.minimum(jnp.maximum(array, -bound), bound).astype(held_as)


def setup_inputs(seed: int = 0) -> dict:
    key_of = jax.random.split(jax.random.key(seed), 3)
    return {
        "log_coef": bell_draw(key_of[0], (SAMPLES, NX, NY), 1.0, 4.0, ((0, 2), (1, 16)), jnp.float32),
        "source": bell_draw(key_of[1], (SAMPLES, NX, NY), 0.1, 0.6, ((0, 2), (1, 16)), jnp.float32),
    }


damping = 0.8


def harmonic(former, latter):
    return 2.0 * former * latter / (former + latter)


def halve(coeffs):
    row_count, col_count = coeffs.shape
    return jnp.mean(coeffs.reshape(row_count // 2, 2, col_count // 2, 2), axis=(1, 3))


def quad_sum(values):
    row_count, col_count = values.shape
    return jnp.sum(values.reshape(row_count // 2, 2, col_count // 2, 2), axis=(1, 3))


def expand(values):
    return jnp.repeat(jnp.repeat(values, 2, axis=0), 2, axis=1)


def side_weights(coeffs):
    shifted = jnp.concatenate([coeffs[:, 1:], coeffs[:, -1:]], axis=1)
    east_face = harmonic(coeffs, shifted)
    west_face = jnp.concatenate([harmonic(coeffs[:, :1], coeffs[:, :1]), east_face[:, :-1]], axis=1)
    return west_face, east_face


def level_weights(coeffs):
    west_face, east_face = side_weights(coeffs)
    padded = jnp.concatenate([coeffs[:1], coeffs, coeffs[-1:]], axis=0)
    return west_face, east_face, harmonic(padded[:-1], padded[1:])


def pad_rows(values):
    return jnp.pad(values, ((1, 1), (0, 0)))


def apply_rows(wide, west_face, east_face, vertical):
    middle = wide[1:-1]
    zero_column = jnp.zeros_like(middle[:, :1])
    west_values = jnp.concatenate([zero_column, middle[:, :-1]], axis=1)
    east_values = jnp.concatenate([middle[:, 1:], zero_column], axis=1)
    north_face = vertical[:-1]
    south_face = vertical[1:]
    diagonal = west_face + east_face + north_face + south_face
    applied = diagonal * middle - (west_face * west_values + east_face * east_values
                                   + north_face * wide[:-2] + south_face * wide[2:])
    return middle, applied, diagonal


def relax_rows(wide, right_side, west_face, east_face, vertical):
    middle, applied, diagonal = apply_rows(wide, west_face, east_face, vertical)
    return middle + damping * (right_side - applied) / diagonal


def vcycle(height, iterate, right_side, ladder):
    weights = ladder[height]
    if height == len(ladder) - 1:
        for repeat in range(COARSE_SWEEPS):
            iterate = relax_rows(pad_rows(iterate), right_side, *weights)
        return iterate
    for repeat in range(2):
        iterate = relax_rows(pad_rows(iterate), right_side, *weights)
    middle, applied, diagonal = apply_rows(pad_rows(iterate), *weights)
    coarse_side = quad_sum(right_side - applied)
    errors = vcycle(height + 1, jnp.zeros_like(coarse_side), coarse_side, ladder)
    iterate = iterate + expand(errors)
    for repeat in range(2):
        iterate = relax_rows(pad_rows(iterate), right_side, *weights)
    return iterate


def one_sample(sample_pair):
    log_field, source_field = sample_pair
    coeffs = jnp.exp(log_field)
    ladder = []
    for height in range(LEVELS):
        if height:
            coeffs = halve(coeffs)
        ladder.append(level_weights(coeffs))
    fine_field = jnp.zeros_like(source_field)
    for repeat in range(VCYCLES):
        fine_field = vcycle(0, fine_field, source_field, ladder)
    coarse_side = quad_sum(source_field)
    coarse = jnp.zeros_like(coarse_side)
    for repeat in range(VCYCLES):
        coarse = vcycle(1, coarse, coarse_side, ladder)
    return fine_field - expand(coarse)


def reference(log_coef, source):
    correction = lax.map(one_sample, (log_coef, source))
    summed = jnp.sum(correction, axis=0)
    squares = jnp.sum(correction * correction, axis=0)
    level_mean = summed / SAMPLES
    level_var = (squares - SAMPLES * level_mean * level_mean) / (SAMPLES - 1)
    return correction, level_mean, level_var
```

```python
import functools

import jax
import jax.numpy as jnp
from jax import lax
from jax.experimental import pallas as pl
from jax.experimental.pallas import tpu as pltpu
from jax.sharding import PartitionSpec as P

CYCLES = 2
SUB = 8
LANE = 128
HALO = (8, 4, 6, 16, 8)
SHIFT = (None, 1, 2, 4, 0)
F32 = jnp.float32


def harmonic(a, b):
    return 2.0 * a * b / (a + b)


def iota(shape, axis):
    return lax.broadcasted_iota(jnp.int32, shape, axis)


def roll(x, shift, axis):
    return pltpu.roll(x, shift % x.shape[axis], axis)


def q_next(x):
    ax = x.ndim - 1
    return jnp.where(iota(x.shape, ax) < 112, roll(x, -16, ax), roll(x, -17, ax))


def q_prev(x):
    ax = x.ndim - 1
    return jnp.where(iota(x.shape, ax) >= 16, roll(x, 16, ax), roll(x, 17, ax))


def east_of(x, k):
    if k == 0:
        return q_next(x)
    ax = x.ndim - 2
    y = roll(x, -k, ax)
    return jnp.where(iota(x.shape, ax) < SUB - k, y, q_next(y))


def west_of(x, k):
    if k == 0:
        return q_prev(x)
    ax = x.ndim - 2
    y = roll(x, k, ax)
    return jnp.where(iota(x.shape, ax) >= k, y, q_prev(y))


def west_edge(shape, k):
    edge = iota(shape, len(shape) - 1) == 0
    if k:
        edge = jnp.logical_and(edge, iota(shape, len(shape) - 2) < k)
    return edge


def east_edge(shape, k):
    edge = iota(shape, len(shape) - 1) == LANE - 1
    if k:
        edge = jnp.logical_and(edge, iota(shape, len(shape) - 2) >= SUB - k)
    return edge


def pair_sum(x, k):
    ax = x.ndim - 2
    if 2 * k == SUB:
        return x + roll(x, k, ax)
    odd = (iota(x.shape, ax) // k) % 2 == 1
    return x + jnp.where(odd, roll(x, k, ax), roll(x, -k, ax))


def swap_bits(tiles, axis, count):
    tiles = list(tiles)
    for k in range(count):
        w = 1 << k
        bit = (iota(tiles[0].shape, axis) // w) % 2 == 1
        for t in range(len(tiles)):
            if t & w == 0:
                a, b = tiles[t], tiles[t | w]
                tiles[t] = jnp.where(bit, roll(b, w, axis), a)
                tiles[t | w] = jnp.where(bit, b, roll(a, -w, axis))
    return tiles


def blocks(lo, hi, size, body):
    count = (hi - lo) // size
    if count > 1:
        lax.fori_loop(0, count, lambda j, c: (body(lo + j * size, size), c)[1], 0)
    elif count == 1:
        body(lo, size)
    rest = (hi - lo) - count * size
    if rest:
        body(lo + count * size, rest)


def kernel(grid_count, own, lc_hbm, src_hbm, corr, mean, var, rawc, raws, b0, c0, v0a, v0b, nf0, w0, m0, e0, d0,
           di0, lev, rc2, rc3, rb2, rv1, rb3, rv0, rv1c, rcorr, send_sem, recv_sem, load_sem):
    me = lax.axis_index("grid")
    samp = lax.axis_index("samp")
    n0 = own[0]
    counter = [0]

    def to_grid(dist, src, dst):
        k = counter[0]
        counter[0] += 1
        target = me + dist
        copy = pltpu.make_async_remote_copy(
            src_ref=src, dst_ref=dst, send_sem=send_sem.at[k], recv_sem=recv_sem.at[k],
            device_id={"grid": target}, device_id_type=pl.DeviceIdType.MESH)
        sends = target >= 0 if dist < 0 else target < grid_count
        source = me - dist
        gets = source < grid_count if dist < 0 else source >= 0
        return copy, sends, gets

    def start(items):
        for copy, sends, gets in items:
            @pl.when(sends)
            def _():
                copy.start()

    def finish(items):
        for copy, sends, gets in items:
            @pl.when(sends)
            def _():
                copy.wait_send()

            @pl.when(gets)
            def _():
                copy.wait_recv()

    h0 = HALO[0]
    load_c = pltpu.make_async_copy(lc_hbm.at[0], rawc.at[pl.ds(h0, n0)], load_sem.at[0])
    load_s = pltpu.make_async_copy(src_hbm.at[0], raws.at[pl.ds(h0, n0)], load_sem.at[1])
    load_c.start()
    load_s.start()

    edge = 2
    @pl.when(jnp.logical_or(me < edge, me >= grid_count - edge))
    def _():
        @pl.when(me == 0)
        def _():
            rawc[pl.ds(0, h0)] = jnp.zeros((h0, rawc.shape[1]), F32)
            raws[pl.ds(0, h0)] = jnp.zeros((h0, rawc.shape[1]), F32)

        @pl.when(me == grid_count - 1)
        def _():
            rawc[pl.ds(h0 + n0, h0)] = jnp.zeros((h0, rawc.shape[1]), F32)
            raws[pl.ds(h0 + n0, h0)] = jnp.zeros((h0, rawc.shape[1]), F32)

        rc2[...] = jnp.ones_like(rc2)
        rc3[...] = jnp.ones_like(rc3)
        for ref in (rb2, rv1, rb3, rv0, rv1c):
            for i in range(ref.shape[0]):
                ref[i] = jnp.zeros(ref.shape[1:], F32)

    barrier = pltpu.get_barrier_semaphore()
    for dist in (-2, -1, 1, 2):
        inside = me + dist >= 0 if dist < 0 else me + dist < grid_count

        @pl.when(inside)
        def _():
            pl.semaphore_signal(barrier, inc=1, device_id={"grid": me + dist}, device_id_type=pl.DeviceIdType.MESH)
    pl.semaphore_signal(barrier, inc=1, device_id={"samp": 1 - samp}, device_id_type=pl.DeviceIdType.MESH)
    below = jnp.minimum(me, 2)
    above = jnp.minimum(grid_count - 1 - me, 2)
    pl.semaphore_wait(barrier, 1 + below + above)

    raw_items = []
    for hbm, raw in ((lc_hbm, rawc), (src_hbm, raws)):
        raw_items.append(to_grid(-1, hbm.at[0, pl.ds(0, h0)], raw.at[pl.ds(h0 + n0, h0)]))
        raw_items.append(to_grid(1, hbm.at[0, pl.ds(n0 - h0, h0)], raw.at[pl.ds(0, h0)]))
    start(raw_items)

    tiles = rawc.shape[1] // LANE
    lane_bits = tiles.bit_length() - 1

    def load_group(raw, out, fn, g):
        base = pl.multiple_of(g * SUB, SUB)
        y = swap_bits([raw[pl.ds(base, SUB), t * LANE:(t + 1) * LANE] for t in range(tiles)], 1, lane_bits)
        for p in range(2):
            z = swap_bits(y[p::2], 0, 3)
            for r in range(SUB):
                out[base + r, p] = fn(z[r])

    def groups(raw, out, fn, lo, hi):
        lax.fori_loop(lo, hi, lambda g, c: (load_group(raw, out, fn, g), c)[1], 0)

    gh, gn = h0 // SUB, n0 // SUB
    load_c.wait()
    groups(rawc, c0, jnp.exp, gh, gh + gn)

    def children(level, j):
        return 2 * (j - HALO[level]) + HALO[level - 1]

    def coarse_coef(level, lo, hi):
        c = lev[level]["c"]

        def body(j, size):
            first = children(level, j)
            if level == 1:
                x = c0[pl.ds(first, 2 * size)].reshape(size, 4, SUB, LANE)
                c[pl.ds(j, size)] = 0.25 * (x[:, 0] + x[:, 1] + x[:, 2] + x[:, 3])
            else:
                x = lev[level - 1]["c"][pl.ds(first, 2 * size)].reshape(size, 2, SUB, LANE)
                c[pl.ds(j, size)] = 0.25 * pair_sum(x[:, 0] + x[:, 1], SHIFT[level - 1])
        blocks(lo, hi, 4, body)

    H = HALO
    for level in (1, 2, 3):
        coarse_coef(level, H[level], H[level] + own[level])
    c2, c3 = lev[2]["c"], lev[3]["c"]
    coef_items = [
        to_grid(-1, c2.at[pl.ds(H[2], H[2])], rc2.at[1]),
        to_grid(1, c2.at[pl.ds(H[2] + own[2] - H[2], H[2])], rc2.at[0]),
        to_grid(-1, c3.at[pl.ds(H[3], own[3])], rc3.at[2]),
        to_grid(-2, c3.at[pl.ds(H[3], own[3])], rc3.at[3]),
        to_grid(1, c3.at[pl.ds(H[3], own[3])], rc3.at[1]),
        to_grid(2, c3.at[pl.ds(H[3], own[3])], rc3.at[0]),
    ]
    start(coef_items)
    load_s.wait()
    groups(raws, b0, lambda x: x, gh, gh + gn)
    finish(raw_items)
    for raw, out, fn in ((rawc, c0, jnp.exp), (raws, b0, lambda x: x)):
        groups(raw, out, fn, 0, gh)
        groups(raw, out, fn, gh + gn, gh + gn + gh)
    coarse_coef(1, 0, H[1])
    coarse_coef(1, H[1] + own[1], 2 * H[1] + own[1])

    def row_mask(level, i, size, value):
        return iota((size, SUB, LANE), 0) + i == value

    def first_row(level):
        return H[level] - me * own[level]

    def end_row(level):
        return H[level] + (grid_count - me) * own[level]

    def inside_rows(level, i, size):
        at = iota((size, SUB, LANE), 0) + i
        return jnp.logical_and(at >= first_row(level), at < end_row(level))

    def vertical(level, c, out, lo, hi):
        def body(i, size):
            a, b = c(i - 1, size), c(i, size)
            top = row_mask(level, i, size, first_row(level))
            bottom = row_mask(level, i, size, end_row(level))
            out(i, size, harmonic(jnp.where(top, b, a), jnp.where(bottom, a, b)))
        blocks(lo, hi, 4, body)

    total0 = n0 + 2 * h0
    for p in range(2):
        def put(i, size, x):
            nf0[pl.ds(i, size), p] = x
        vertical(0, lambda i, size: c0[pl.ds(i, size), p], put, 1, total0)

    def weights0(i, size):
        a, b = c0[pl.ds(i, size), 0], c0[pl.ds(i, size), 1]
        we, ee = west_edge(a.shape, 1), east_edge(a.shape, 1)
        wf = harmonic(jnp.where(we, a, west_of(b, 1)), a)
        mf = harmonic(a, b)
        ef = harmonic(b, jnp.where(ee, b, east_of(a, 1)))
        w0[pl.ds(i, size)] = jnp.where(we, 0.0, wf)
        m0[pl.ds(i, size)] = mf
        e0[pl.ds(i, size)] = jnp.where(ee, 0.0, ef)
        inside = inside_rows(0, i, size)
        for p, (x, y) in enumerate(((wf, mf), (mf, ef))):
            d = x + y + nf0[pl.ds(i, size), p] + nf0[pl.ds(i + 1, size), p]
            d0[pl.ds(i, size), p] = d
            di0[pl.ds(i, size), p] = jnp.where(inside, 0.8 / d, 0.0)
    blocks(1, total0 - 1, 2, weights0)

    def coarse_weights(level):
        L = lev[level]
        k = SHIFT[level]
        total = own[level] + 2 * H[level]

        def put(i, size, x):
            L["nf"][pl.ds(i, size)] = x
        vertical(level, lambda i, size: L["c"][pl.ds(i, size)], put, 1, total)

        def body(i, size):
            c = L["c"][pl.ds(i, size)]
            we, ee = west_edge(c.shape, k), east_edge(c.shape, k)
            wf = harmonic(jnp.where(we, c, west_of(c, k)), c)
            ef = harmonic(c, jnp.where(ee, c, east_of(c, k)))
            L["w"][pl.ds(i, size)] = jnp.where(we, 0.0, wf)
            L["e"][pl.ds(i, size)] = jnp.where(ee, 0.0, ef)
            d = wf + ef + L["nf"][pl.ds(i, size)] + L["nf"][pl.ds(i + 1, size)]
            L["d"][pl.ds(i, size)] = d
            L["di"][pl.ds(i, size)] = jnp.where(inside_rows(level, i, size), 0.8 / d, 0.0)
        blocks(1, total - 1, 2, body)

    coarse_weights(1)

    def around0(v, i, size):
        sums = []
        u = [v[pl.ds(i, size), p] for p in range(2)]
        mid = m0[pl.ds(i, size)]
        sums.append(w0[pl.ds(i, size)] * west_of(u[1], 1) + mid * u[1])
        sums.append(mid * u[0] + e0[pl.ds(i, size)] * east_of(u[0], 1))
        for p in range(2):
            sums[p] = sums[p] + (nf0[pl.ds(i, size), p] * v[pl.ds(i - 1, size), p]
                                 + nf0[pl.ds(i + 1, size), p] * v[pl.ds(i + 1, size), p])
        return u, sums

    def sweep0(src, dst, halo):
        def body(i, size):
            u, sums = around0(src, i, size)
            for p in range(2):
                dst[pl.ds(i, size), p] = 0.2 * u[p] + di0[pl.ds(i, size), p] * (b0[pl.ds(i, size), p] + sums[p])
        blocks(h0 - halo, h0 + n0 + halo, 2, body)

    def restrict0(v, out, halo):
        def body(j, size):
            i = children(1, j)
            u, sums = around0(v, i, 2 * size)
            r = 0.0
            for p in range(2):
                r = r + (b0[pl.ds(i, 2 * size), p] - d0[pl.ds(i, 2 * size), p] * u[p] + sums[p])
            r = r.reshape(size, 2, SUB, LANE)
            out[0, pl.ds(j, size)] = r[:, 0] + r[:, 1]
        blocks(H[1] - halo, H[1] + own[1] + halo, 1, body)

    def around(level, v, pr, i, size):
        L = lev[level]
        k = SHIFT[level]
        u = v[pr, pl.ds(i, size)]
        s = (L["w"][pl.ds(i, size)] * west_of(u, k) + L["e"][pl.ds(i, size)] * east_of(u, k)
             + L["nf"][pl.ds(i, size)] * v[pr, pl.ds(i - 1, size)]
             + L["nf"][pl.ds(i + 1, size)] * v[pr, pl.ds(i + 1, size)])
        return u, s

    def sweep(level, src, dst, halo):
        L = lev[level]

        def body(i, size):
            for pr in range(2):
                u, s = around(level, src, pr, i, size)
                dst[pr, pl.ds(i, size)] = 0.2 * u + L["di"][pl.ds(i, size)] * (L["b"][pr, pl.ds(i, size)] + s)
        blocks(H[level] - halo, H[level] + own[level] + halo, 2, body)

    def first_sweep(level, dst, halo):
        L = lev[level]

        def body(i, size):
            for pr in range(2):
                dst[pr, pl.ds(i, size)] = L["di"][pl.ds(i, size)] * L["b"][pr, pl.ds(i, size)]
        blocks(H[level] - halo, H[level] + own[level] + halo, 4, body)

    def restrict(level, v, halo):
        L = lev[level]

        def body(j, size):
            i = children(level + 1, j)
            for pr in range(2):
                u, s = around(level, v, pr, i, 2 * size)
                r = L["b"][pr, pl.ds(i, 2 * size)] - L["d"][pl.ds(i, 2 * size)] * u + s
                r = r.reshape(size, 2, SUB, LANE)
                lev[level + 1]["b"][pr, pl.ds(j, size)] = pair_sum(r[:, 0] + r[:, 1], SHIFT[level])
        n = level + 1
        blocks(H[n] - halo, H[n] + own[n] + halo, 1, body)

    def correct(level, v, e, halo):
        n = level + 1

        def body(j, size):
            i = children(n, j)
            for pr in range(2):
                x = e[pr, pl.ds(j, size)]
                for r in range(2):
                    for q in range(size):
                        v[pr, i + 2 * q + r] = v[pr, i + 2 * q + r] + x[q]
        blocks(H[n] - halo, H[n] + own[n] + halo, 2, body)

    b1 = lev[1]["b"]

    def restrict_source(j, size):
        x = b0[pl.ds(children(1, j), 2 * size)].reshape(size, 4, SUB, LANE)
        b1[1, pl.ds(j, size)] = x[:, 0] + x[:, 1] + x[:, 2] + x[:, 3]
    blocks(0, own[1] + 2 * H[1], 2, restrict_source)

    for cycle in range(CYCLES):
        v1a, v1b = lev[1]["va"], lev[1]["vb"]
        if cycle == 0:
            def first0(i, size):
                for p in range(2):
                    v0b[pl.ds(i, size), p] = di0[pl.ds(i, size), p] * b0[pl.ds(i, size), p]
            blocks(h0 - 7, h0 + n0 + 7, 2, first0)
        else:
            sweep0(v0a, v0b, 7)
        sweep0(v0b, v0a, 6)
        restrict0(v0a, b1, 2)
        if cycle == 0:
            first_sweep(1, v1b, 3)
        else:
            def clear(i, size):
                v1a[0, pl.ds(i, size)] = jnp.zeros((size, SUB, LANE), F32)
            blocks(0, own[1] + 2 * H[1], 4, clear)
            sweep(1, v1a, v1b, 3)
        sweep(1, v1b, v1a, 2)
        restrict(1, v1a, 0)
        b2 = lev[2]["b"]
        items = [
            to_grid(-1, b2.at[:, pl.ds(H[2], 5)], rb2.at[cycle, 1]),
            to_grid(1, b2.at[:, pl.ds(H[2] + own[2] - 5, 5)], rb2.at[cycle, 0]),
            to_grid(-1, v1a.at[:, pl.ds(H[1], 3)], rv1.at[cycle, 1]),
            to_grid(1, v1a.at[:, pl.ds(H[1] + own[1] - 3, 3)], rv1.at[cycle, 0]),
        ]
        start(items)
        if cycle == 0:
            finish(coef_items)
            c2[pl.ds(0, H[2])] = rc2[0]
            c2[pl.ds(H[2] + own[2], H[2])] = rc2[1]
            for s in range(4):
                at = (0, own[3], H[3] + own[3], H[3] + 2 * own[3])[s]
                c3[pl.ds(at, own[3])] = rc3[s]
            coarse_coef(4, 0, own[4] + 2 * H[4])
            for level in (2, 3, 4):
                coarse_weights(level)
        finish(items)
        for pr in range(2):
            b2[pr, pl.ds(H[2] - 5, 5)] = rb2[cycle, 0, pr]
            b2[pr, pl.ds(H[2] + own[2], 5)] = rb2[cycle, 1, pr]
            v1a[pr, pl.ds(H[1] - 3, 3)] = rv1[cycle, 0, pr]
            v1a[pr, pl.ds(H[1] + own[1], 3)] = rv1[cycle, 1, pr]
        v2a, v2b = lev[2]["va"], lev[2]["vb"]
        first_sweep(2, v2b, 5)
        sweep(2, v2b, v2a, 4)
        restrict(2, v2a, 0)
        b3 = lev[3]["b"]
        mine = b3.at[:, pl.ds(H[3], own[3])]
        items = [
            to_grid(-1, mine, rb3.at[cycle, 2]),
            to_grid(-2, mine, rb3.at[cycle, 3]),
            to_grid(1, mine, rb3.at[cycle, 1]),
            to_grid(2, mine, rb3.at[cycle, 0]),
        ]
        start(items)
        finish(items)
        for s in range(4):
            at = (0, own[3], H[3] + own[3], H[3] + 2 * own[3])[s]
            for pr in range(2):
                b3[pr, pl.ds(at, own[3])] = rb3[cycle, s, pr]
        v3a, v3b = lev[3]["va"], lev[3]["vb"]
        v4a, v4b = lev[4]["va"], lev[4]["vb"]
        first_sweep(3, v3b, 13)
        sweep(3, v3b, v3a, 12)
        restrict(3, v3a, 5)
        first_sweep(4, v4b, 5)
        sweep(4, v4b, v4a, 4)
        sweep(4, v4a, v4b, 3)
        sweep(4, v4b, v4a, 2)
        correct(3, v3a, v4a, 2)
        sweep(3, v3a, v3b, 3)
        sweep(3, v3b, v3a, 2)
        correct(2, v2a, v3a, 2)
        sweep(2, v2a, v2b, 3)
        sweep(2, v2b, v2a, 2)
        correct(1, v1a, v2a, 2)
        sweep(1, v1a, v1b, 2)
        sweep(1, v1b, v1a, 1)

        def correct0(j, size):
            i = children(1, j)
            x = v1a[0, pl.ds(j, size)]
            for q in range(size):
                for r in range(2):
                    for p in range(2):
                        v0a[i + 2 * q + r, p] = v0a[i + 2 * q + r, p] + x[q]
        blocks(H[1] - 1, H[1] + own[1] + 1, 2, correct0)
        sweep0(v0a, v0b, 1)
        sweep0(v0b, v0a, 0)
        if cycle < CYCLES - 1:
            h1 = H[1]
            items = [
                to_grid(-1, v0a.at[pl.ds(h0, h0)], rv0.at[1]),
                to_grid(1, v0a.at[pl.ds(n0, h0)], rv0.at[0]),
                to_grid(-1, v1a.at[1, pl.ds(h1, h1)], rv1c.at[1]),
                to_grid(1, v1a.at[1, pl.ds(own[1], h1)], rv1c.at[0]),
            ]
            start(items)
            finish(items)

            def take0(i, size):
                v0a[pl.ds(i, size)] = rv0[0, pl.ds(i, size)]
                v0a[pl.ds(h0 + n0 + i, size)] = rv0[1, pl.ds(i, size)]
            blocks(0, h0, 4, take0)
            v1a[1, pl.ds(0, h1)] = rv1c[0]
            v1a[1, pl.ds(h1 + own[1], h1)] = rv1c[1]

    half = corr.shape[1] // 2
    first = counter[0]

    def corr_copy(g):
        base = pl.multiple_of(g * SUB, SUB)
        there = pl.multiple_of((1 - samp) * half, LANE)
        return pltpu.make_async_remote_copy(
            src_ref=corr.at[pl.ds(base, SUB), pl.ds(there, half)], dst_ref=rcorr.at[pl.ds(base, SUB)],
            send_sem=send_sem.at[first + g], recv_sem=recv_sem.at[first + g],
            device_id={"samp": 1 - samp}, device_id_type=pl.DeviceIdType.MESH)

    v1a = lev[1]["va"]

    def emit(g, carry):
        base = pl.multiple_of(g * SUB, SUB)
        y = [None] * tiles
        cs = [v1a[1, H[1] + g * (SUB // 2) + r] for r in range(SUB // 2)]
        for p in range(2):
            z = [v0a[h0 + base + r, p] - cs[r // 2] for r in range(SUB)]
            y[p::2] = swap_bits(z, 0, 3)
        y = swap_bits(y, 1, lane_bits)
        for t in range(tiles):
            corr[pl.ds(base, SUB), t * LANE:(t + 1) * LANE] = y[t]
        corr_copy(g).start()
        return carry
    lax.fori_loop(0, gn, emit, 0)

    def combine(g, carry):
        base = pl.multiple_of(g * SUB, SUB)
        corr_copy(g).wait()
        here = pl.multiple_of(samp * half, LANE)
        a = corr[pl.ds(base, SUB), pl.ds(here, half)]
        b = rcorr[pl.ds(base, SUB)]
        m = (a + b) / 2.0
        mean[pl.ds(base, SUB)] = m
        var[pl.ds(base, SUB)] = a * a + b * b - 2.0 * m * m
        return carry
    lax.fori_loop(0, gn, combine, 0)


NAMES = ("c", "nf", "w", "e", "d", "di", "b", "va", "vb")


def entry(grid_count, own, *refs):
    refs = list(refs)
    head, rest = refs[:17], refs[17:]
    lev = {}
    for level in range(1, 5):
        lev[level] = dict(zip(NAMES, rest[:len(NAMES)]))
        rest = rest[len(NAMES):]
    kernel(grid_count, own, *head, lev, *rest)


def local(grid_count, log_coef, source):
    _, n0, cols = log_coef.shape
    own = tuple(n0 >> level for level in range(5))
    assert cols == 2 * SUB * LANE and own[4] * 2 == SUB

    def vm(*shape):
        return pltpu.VMEM(shape + (SUB, LANE), F32)

    t0 = n0 + 2 * HALO[0]
    scratch = [pltpu.VMEM((t0, cols), F32)] * 2
    scratch += [vm(t0, 2)] * 5 + [vm(t0)] * 3 + [vm(t0, 2)] * 2
    for level in range(1, 5):
        t = own[level] + 2 * HALO[level]
        scratch += [vm(t)] * 6 + [vm(2, t)] * 3
    copies = 14 + CYCLES * 8 + n0 // SUB
    scratch += [
        vm(2, HALO[2]), vm(4, own[3]), vm(CYCLES, 2, 2, 5), vm(CYCLES, 2, 2, 3), vm(CYCLES, 4, 2, own[3]),
        vm(2, HALO[0], 2), vm(2, HALO[1]), pltpu.VMEM((n0, cols // 2), F32),
        pltpu.SemaphoreType.DMA((copies,)), pltpu.SemaphoreType.DMA((copies,)), pltpu.SemaphoreType.DMA((2,)),
    ]
    out = [jax.ShapeDtypeStruct((n0, cols), F32)] + [jax.ShapeDtypeStruct((n0, cols // 2), F32)] * 2
    corr, mean, var = pl.pallas_call(
        functools.partial(entry, grid_count, own),
        out_shape=out,
        in_specs=[pl.BlockSpec(memory_space=pl.ANY)] * 2,
        out_specs=[pl.BlockSpec(memory_space=pltpu.VMEM)] * 3,
        scratch_shapes=scratch,
        compiler_params=pltpu.CompilerParams(
            collective_id=0, has_side_effects=True, vmem_limit_bytes=48 * 1024 * 1024),
    )(log_coef, source)
    return corr[None], mean, var


def solution(mesh):
    spec = P("samp", "grid", None)
    return jax.shard_map(
        functools.partial(local, mesh.shape["grid"]), mesh=mesh, in_specs=(spec, spec),
        out_specs=(spec, P("grid", "samp"), P("grid", "samp")), check_vma=False)
```

```python
import functools

import jax
import jax.numpy as jnp
from jax import lax
from jax.experimental import pallas as pl
from jax.experimental.pallas import tpu as pltpu
from jax.sharding import PartitionSpec as P

CYCLES = 2
LEVELS = 5
SUB = 8
LANE = 128
PAD = 8
HALO = (8, 4, 8, 16, 8)
ROLLED = (True, True, False, False, False)
F32 = jnp.float32


def harmonic(a, b):
    return 2.0 * a * b / (a + b)


def iota(axis):
    return lax.broadcasted_iota(jnp.int32, (SUB, LANE), axis)


def roll(x, shift, axis):
    return pltpu.roll(x, shift % x.shape[axis], axis)


def q_next(x):
    return jnp.where(iota(1) < 112, roll(x, -16, 1), roll(x, -17, 1))


def q_prev(x):
    return jnp.where(iota(1) >= 16, roll(x, 16, 1), roll(x, 17, 1))


def swap_bits(tiles, count):
    tiles = list(tiles)
    for k in range(count):
        w = 1 << k
        bit = (iota(1) // w) % 2 == 1
        for t in range(len(tiles)):
            if t & w == 0:
                a, b = tiles[t], tiles[t | w]
                tiles[t] = jnp.where(bit, roll(b, w, 1), a)
                tiles[t | w] = jnp.where(bit, b, roll(a, -w, 1))
    return tiles


def kernel(grid_count, own, rows, lc_hbm, src_hbm, corr, mean, var, rawc, raws, lev, rc2, rc3, sb1, rv1, rb2, rb3, rv0,
           sc1, rv1c, rcorr, send_sem, recv_sem, load_sem):
    me = lax.axis_index("grid")
    samp = lax.axis_index("samp")
    n0 = own[0]
    counter = [0]
    planes = [lev[level]["c"].shape[0] for level in range(LEVELS)]
    H = HALO
    h0 = H[0]

    def rd(i):
        return pl.ds(PAD + i, SUB)

    def groups(level, body, lo=0, hi=None):
        hi = rows[level] // SUB if hi is None else hi
        if ROLLED[level]:
            def step(g, carry):
                body(pl.multiple_of(g * SUB, SUB))
                return carry
            lax.fori_loop(lo, hi, step, 0)
        else:
            for g in range(lo, hi):
                body(g * SUB)

    def to_grid(dist, src, dst):
        k = counter[0]
        counter[0] += 1
        target = me + dist
        copy = pltpu.make_async_remote_copy(
            src_ref=src, dst_ref=dst, send_sem=send_sem.at[k], recv_sem=recv_sem.at[k],
            device_id={"grid": target}, device_id_type=pl.DeviceIdType.MESH)
        sends = target >= 0 if dist < 0 else target < grid_count
        source = me - dist
        gets = source < grid_count if dist < 0 else source >= 0
        return copy, sends, gets

    def start(items):
        for copy, sends, gets in items:
            @pl.when(sends)
            def _():
                copy.start()

    def finish(items):
        for copy, sends, gets in items:
            @pl.when(sends)
            def _():
                copy.wait_send()

            @pl.when(gets)
            def _():
                copy.wait_recv()

    load_c = pltpu.make_async_copy(lc_hbm.at[0], rawc.at[pl.ds(h0, n0)], load_sem.at[0])
    load_s = pltpu.make_async_copy(src_hbm.at[0], raws.at[pl.ds(h0, n0)], load_sem.at[1])
    load_c.start()
    load_s.start()

    edge = 2
    @pl.when(jnp.logical_or(me < edge, me >= grid_count - edge))
    def _():
        @pl.when(me == 0)
        def _():
            rawc[pl.ds(0, h0)] = jnp.zeros((h0, rawc.shape[1]), F32)
            raws[pl.ds(0, h0)] = jnp.zeros((h0, rawc.shape[1]), F32)

        @pl.when(me == grid_count - 1)
        def _():
            rawc[pl.ds(h0 + n0, h0)] = jnp.zeros((h0, rawc.shape[1]), F32)
            raws[pl.ds(h0 + n0, h0)] = jnp.zeros((h0, rawc.shape[1]), F32)

        for ref in (rc2, rc3):
            for i in range(ref.shape[0]):
                ref[i] = jnp.ones(ref.shape[1:], F32)
        for ref in (rv1, rb2, rb3, rv0, rv1c):
            for i in range(ref.shape[0]):
                ref[i] = jnp.zeros(ref.shape[1:], F32)

    barrier = pltpu.get_barrier_semaphore()
    for dist in (-2, -1, 1, 2):
        inside = me + dist >= 0 if dist < 0 else me + dist < grid_count

        @pl.when(inside)
        def _():
            pl.semaphore_signal(barrier, inc=1, device_id={"grid": me + dist}, device_id_type=pl.DeviceIdType.MESH)
    pl.semaphore_signal(barrier, inc=1, device_id={"samp": 1 - samp}, device_id_type=pl.DeviceIdType.MESH)
    below = jnp.minimum(me, 2)
    above = jnp.minimum(grid_count - 1 - me, 2)
    pl.semaphore_wait(barrier, 1 + below + above)

    raw_items = []
    for hbm, raw in ((lc_hbm, rawc), (src_hbm, raws)):
        raw_items.append(to_grid(-1, hbm.at[0, pl.ds(0, h0)], raw.at[pl.ds(h0 + n0, h0)]))
        raw_items.append(to_grid(1, hbm.at[0, pl.ds(n0 - h0, h0)], raw.at[pl.ds(0, h0)]))
    start(raw_items)

    tiles = rawc.shape[1] // LANE
    lane_bits = tiles.bit_length() - 1

    def split(raw, out, fn, lo, hi):
        def step(g, carry):
            base = pl.multiple_of(g * SUB, SUB)
            y = swap_bits([raw[pl.ds(base, SUB), t * LANE:(t + 1) * LANE] for t in range(tiles)], lane_bits)
            for r in range(tiles):
                out[r, rd(base)] = fn(y[r])
            return carry
        lax.fori_loop(lo, hi, step, 0)

    def same(x):
        return x

    def children(level, j):
        return 2 * (j - H[level]) + H[level - 1]

    def gather_pairs(level, out, starts, scale=None):
        t = lev[level - 1]["t"]
        for k in range(planes[level]):
            for j in starts:
                first = PAD + children(level, j)
                x = t[k, pl.ds(first, SUB, stride=2)] + t[k, pl.ds(first + 1, SUB, stride=2)]
                out[k, rd(j)] = x if scale is None else scale * x

    def reduce_field(level, field, out, starts, lo, hi, scale=None):
        t = lev[level - 1]["t"]

        def body(i):
            for k in range(planes[level]):
                t[k, rd(i)] = field[2 * k, rd(i)] + field[2 * k + 1, rd(i)]
        groups(level - 1, body, lo, hi)
        gather_pairs(level, out, starts, scale)

    def own_starts(level):
        return range(H[level], H[level] + own[level], SUB)

    def all_starts(level):
        return range(0, rows[level], SUB)

    gh, gn = h0 // SUB, n0 // SUB
    c0, b0 = lev[0]["c"], lev[0]["b"].at[0]
    load_c.wait()
    split(rawc, c0, jnp.exp, gh, gh + gn)
    reduce_field(1, c0, lev[1]["c"], own_starts(1), gh, gh + gn, 0.25)
    reduce_field(2, lev[1]["c"], lev[2]["c"], own_starts(2), 0, None, 0.25)
    reduce_field(3, lev[2]["c"], lev[3]["c"], own_starts(3), 1, 3, 0.25)
    c2, c3 = lev[2]["c"], lev[3]["c"]

    def edges(ref, level):
        at = PAD + H[level]
        return pl.ds(at, SUB), pl.ds(at + own[level] - SUB, SUB)

    top2, bottom2 = edges(c2, 2)
    mine3 = pl.ds(PAD + H[3], own[3])
    coef_items = [
        to_grid(-1, c2.at[:, top2], rc2.at[1]),
        to_grid(1, c2.at[:, bottom2], rc2.at[0]),
        to_grid(-1, c3.at[:, mine3], rc3.at[2]),
        to_grid(-2, c3.at[:, mine3], rc3.at[3]),
        to_grid(1, c3.at[:, mine3], rc3.at[1]),
        to_grid(2, c3.at[:, mine3], rc3.at[0]),
    ]
    start(coef_items)
    load_s.wait()
    split(raws, b0, same, gh, gh + gn)
    finish(raw_items)
    for raw, out, fn in ((rawc, c0, jnp.exp), (raws, b0, same)):
        split(raw, out, fn, 0, gh)
        split(raw, out, fn, gh + gn, gh + gn + gh)
    reduce_field(1, c0, lev[1]["c"], all_starts(1), 0, None, 0.25)

    def weights(level):
        L = lev[level]
        R = planes[level]
        c = L["c"]
        first = H[level] - me * own[level]
        end = H[level] + (grid_count - me) * own[level]

        def vertical(i):
            at = iota(0) + i
            for r in range(R):
                a, b = c[r, rd(i - 1)], c[r, rd(i)]
                L["nf"][r, rd(i)] = harmonic(jnp.where(at == first, b, a), jnp.where(at == end, a, b))
        groups(level, vertical)

        def body(i):
            at = iota(0) + i
            inside = jnp.logical_and(at >= first, at < end)
            u = [c[r, rd(i)] for r in range(R)]
            we, ee = iota(1) == 0, iota(1) == LANE - 1
            faces = [harmonic(jnp.where(we, u[0], q_prev(u[-1])), u[0])]
            faces += [harmonic(u[r - 1], u[r]) for r in range(1, R)]
            faces += [harmonic(u[-1], jnp.where(ee, u[-1], q_next(u[0])))]
            for r in range(R):
                d = faces[r] + faces[r + 1] + L["nf"][r, rd(i)] + L["nf"][r, rd(i + 1)]
                L["d"][r, rd(i)] = d
                L["di"][r, rd(i)] = jnp.where(inside, 0.8 / d, 0.0)
            for r in range(R + 1):
                edge = we if r == 0 else ee
                L["hf"][r, rd(i)] = jnp.where(edge, 0.0, faces[r]) if r in (0, R) else faces[r]
        groups(level, body)

    def around(level, v, i, out):
        L = lev[level]
        R = planes[level]
        count = v.shape[0]
        prev, here, first, west = [], [], [], []
        for pr in range(count):
            first.append(v[pr, 0, rd(i)])
            west.append(q_prev(v[pr, R - 1, rd(i)]))
        here = list(first)
        for r in range(R):
            wf, ef = L["hf"][r, rd(i)], L["hf"][r + 1, rd(i)]
            nf, sf = L["nf"][r, rd(i)], L["nf"][r, rd(i + 1)]
            for pr in range(count):
                after = v[pr, r + 1, rd(i)] if r + 1 < R else None
                east = after if r + 1 < R else q_next(first[pr])
                total = (wf * west[pr] + ef * east) + (nf * v[pr, r, rd(i - 1)] + sf * v[pr, r, rd(i + 1)])
                out(pr, r, here[pr], total)
                west[pr], here[pr] = here[pr], after

    def sweep(level, src, dst, lo=0, hi=None):
        L = lev[level]

        def body(i):
            def out(pr, r, u, total):
                dst[pr, r, rd(i)] = 0.2 * u + L["di"][r, rd(i)] * (L["b"][pr, r, rd(i)] + total)
            around(level, src, i, out)
        groups(level, body, lo, hi)

    def first_sweep(level, dst):
        L = lev[level]

        def body(i):
            for r in range(planes[level]):
                for pr in range(dst.shape[0]):
                    dst[pr, r, rd(i)] = L["di"][r, rd(i)] * L["b"][pr, r, rd(i)]
        groups(level, body)

    def restrict(level, v, starts):
        L = lev[level]
        t2 = (L["t"], L["t2"]) if level else (L["t"],)

        def body(i):
            held = {}

            def out(pr, r, u, total):
                x = L["b"][pr, r, rd(i)] - L["d"][r, rd(i)] * u + total
                if r % 2 == 0:
                    held[pr] = x
                else:
                    t2[pr][r // 2, rd(i)] = held[pr] + x
            around(level, v, i, out)
        groups(level, body)
        for pr in range(v.shape[0]):
            out = lev[level + 1]["b"]
            for k in range(planes[level + 1]):
                for j in starts:
                    first = PAD + children(level + 1, j)
                    out[pr, k, rd(j)] = (t2[pr][k, pl.ds(first, SUB, stride=2)]
                                         + t2[pr][k, pl.ds(first + 1, SUB, stride=2)])

    def correct(level, v, e, starts, pairs, sign=1.0):
        def body(k):
            for pr, pe in pairs:
                for j in starts:
                    x = e[pe, k, rd(j)]
                    first = PAD + children(level + 1, j)
                    for r in range(2):
                        for h in range(2):
                            at = pl.ds(first + h, SUB, stride=2)
                            y = v[pr, 2 * k + r, at]
                            v[pr, 2 * k + r, at] = y + x if sign > 0 else y - x
        if ROLLED[level]:
            lax.fori_loop(0, planes[level + 1], lambda k, c: (body(k), c)[1], 0)
        else:
            for k in range(planes[level + 1]):
                body(k)

    weights(0)
    weights(1)
    b1, v1a, v1b = lev[1]["b"], lev[1]["va"], lev[1]["vb"]
    v0a, v0b = lev[0]["va"], lev[0]["vb"]
    reduce_field(1, b0, b1.at[1], all_starts(1), 0, None)
    h1, n1 = H[1], own[1]
    R1 = planes[1]
    both = ((0, 0), (1, 1))

    for cycle in range(CYCLES):
        if cycle == 0:
            first_sweep(0, v0b)
        else:
            sweep(0, v0a, v0b)
        sweep(0, v0b, v0a)
        restrict(0, v0a, all_starts(1))
        if cycle == 0:
            first_sweep(1, v1b)
        else:
            def clear(i):
                for r in range(R1):
                    v1a[0, r, rd(i)] = jnp.zeros((SUB, LANE), F32)
            groups(1, clear)
            sweep(1, v1a, v1b)
        sweep(1, v1b, v1a)
        restrict(1, v1a, own_starts(2))
        b2 = lev[2]["b"]
        for pr in range(2):
            for r in range(R1):
                sb1[cycle, 0, pr, r] = v1a[pr, r, rd(h1)]
                sb1[cycle, 1, pr, r] = v1a[pr, r, rd(h1 + n1 - SUB)]
        items = [
            to_grid(-1, b2.at[:, :, top2], rb2.at[cycle, 1]),
            to_grid(1, b2.at[:, :, bottom2], rb2.at[cycle, 0]),
            to_grid(-1, sb1.at[cycle, 0], rv1.at[cycle, 1]),
            to_grid(1, sb1.at[cycle, 1], rv1.at[cycle, 0]),
        ]
        start(items)
        if cycle == 0:
            finish(coef_items)
            for r in range(planes[2]):
                c2[r, rd(0)] = rc2[0, r]
                c2[r, rd(H[2] + own[2])] = rc2[1, r]
            for s, at in enumerate((0, SUB, H[3] + SUB, H[3] + 2 * SUB)):
                for r in range(planes[3]):
                    c3[r, rd(at)] = rc3[s, r]
            reduce_field(4, c3, lev[4]["c"], all_starts(4), 0, None, 0.25)
            for level in (2, 3, 4):
                weights(level)
        finish(items)
        for pr in range(2):
            for r in range(planes[2]):
                b2[pr, r, rd(0)] = rb2[cycle, 0, pr, r]
                b2[pr, r, rd(H[2] + own[2])] = rb2[cycle, 1, pr, r]
            for r in range(R1):
                v1a[pr, r, pl.ds(PAD, h1)] = rv1[cycle, 0, pr, r, SUB - h1:, :]
                v1a[pr, r, pl.ds(PAD + h1 + n1, h1)] = rv1[cycle, 1, pr, r, :h1, :]
        v2a, v2b = lev[2]["va"], lev[2]["vb"]
        first_sweep(2, v2b)
        sweep(2, v2b, v2a)
        restrict(2, v2a, own_starts(3))
        b3 = lev[3]["b"]
        mine = b3.at[:, :, mine3]
        items = [
            to_grid(-1, mine, rb3.at[cycle, 2]),
            to_grid(-2, mine, rb3.at[cycle, 3]),
            to_grid(1, mine, rb3.at[cycle, 1]),
            to_grid(2, mine, rb3.at[cycle, 0]),
        ]
        start(items)
        finish(items)
        for s, at in enumerate((0, SUB, H[3] + SUB, H[3] + 2 * SUB)):
            for pr in range(2):
                for r in range(planes[3]):
                    b3[pr, r, rd(at)] = rb3[cycle, s, pr, r]
        v3a, v3b = lev[3]["va"], lev[3]["vb"]
        v4a, v4b = lev[4]["va"], lev[4]["vb"]
        first_sweep(3, v3b)
        sweep(3, v3b, v3a)
        restrict(3, v3a, all_starts(4))
        first_sweep(4, v4b)
        sweep(4, v4b, v4a)
        sweep(4, v4a, v4b)
        sweep(4, v4b, v4a)
        correct(3, v3a, v4a, all_starts(4), both)
        sweep(3, v3a, v3b)
        sweep(3, v3b, v3a)
        correct(2, v2a, v3a, (H[3] - 4, H[3] + 4), both)
        sweep(2, v2a, v2b)
        sweep(2, v2b, v2a)
        correct(1, v1a, v2a, (H[2] - 2, H[2] + 6, H[2] + 14), both)
        sweep(1, v1a, v1b)
        sweep(1, v1b, v1a)
        correct(0, v0a, v1a, all_starts(1), ((0, 0),))
        sweep(0, v0a, v0b)
        sweep(0, v0b, v0a, gh, gh + gn)
        if cycle < CYCLES - 1:
            for r in range(R1):
                sc1[0, r] = v1a[1, r, rd(h1)]
                sc1[1, r] = v1a[1, r, rd(h1 + n1 - SUB)]
            top0, bottom0 = edges(v0a, 0)
            items = [
                to_grid(-1, v0a.at[0, :, top0], rv0.at[1]),
                to_grid(1, v0a.at[0, :, bottom0], rv0.at[0]),
                to_grid(-1, sc1.at[0], rv1c.at[1]),
                to_grid(1, sc1.at[1], rv1c.at[0]),
            ]
            start(items)
            finish(items)
            for r in range(planes[0]):
                v0a[0, r, rd(0)] = rv0[0, r]
                v0a[0, r, rd(h0 + n0)] = rv0[1, r]
            for r in range(R1):
                v1a[1, r, pl.ds(PAD, h1)] = rv1c[0, r, SUB - h1:, :]
                v1a[1, r, pl.ds(PAD + h1 + n1, h1)] = rv1c[1, r, :h1, :]
    correct(0, v0a, v1a, own_starts(1), ((0, 1),), -1.0)

    half = corr.shape[1] // 2
    first = counter[0]

    def corr_copy(g):
        base = pl.multiple_of(g * SUB, SUB)
        there = pl.multiple_of((1 - samp) * half, LANE)
        return pltpu.make_async_remote_copy(
            src_ref=corr.at[pl.ds(base, SUB), pl.ds(there, half)], dst_ref=rcorr.at[pl.ds(base, SUB)],
            send_sem=send_sem.at[first + g], recv_sem=recv_sem.at[first + g],
            device_id={"samp": 1 - samp}, device_id_type=pl.DeviceIdType.MESH)

    def emit(g, carry):
        base = pl.multiple_of(g * SUB, SUB)
        y = swap_bits([v0a[0, r, rd(h0 + base)] for r in range(tiles)], lane_bits)
        for t in range(tiles):
            corr[pl.ds(base, SUB), t * LANE:(t + 1) * LANE] = y[t]
        corr_copy(g).start()
        return carry
    lax.fori_loop(0, gn, emit, 0)

    def combine(g, carry):
        base = pl.multiple_of(g * SUB, SUB)
        corr_copy(g).wait()
        here = pl.multiple_of(samp * half, LANE)
        a = corr[pl.ds(base, SUB), pl.ds(here, half)]
        b = rcorr[pl.ds(base, SUB)]
        m = (a + b) / 2.0
        mean[pl.ds(base, SUB)] = m
        var[pl.ds(base, SUB)] = a * a + b * b - 2.0 * m * m
        return carry
    lax.fori_loop(0, gn, combine, 0)


NAMES = ("c", "nf", "hf", "d", "di", "t", "t2", "b", "va", "vb")


def entry(grid_count, own, rows, *refs):
    refs = list(refs)
    head, rest = refs[:7], refs[7:]
    lev = {}
    for level in range(LEVELS):
        lev[level] = dict(zip(NAMES, rest[:len(NAMES)]))
        rest = rest[len(NAMES):]
    kernel(grid_count, own, rows, *head, lev, *rest)


def local(grid_count, log_coef, source):
    _, n0, cols = log_coef.shape
    own = tuple(n0 >> level for level in range(LEVELS))
    rows = tuple(-(-(own[level] + 2 * HALO[level]) // SUB) * SUB for level in range(LEVELS))
    assert cols == LANE << (LEVELS - 1) and own[LEVELS - 1] * 2 == SUB

    def vm(*shape):
        return pltpu.VMEM(shape + (LANE,), F32)

    scratch = [pltpu.VMEM((n0 + 2 * HALO[0], cols), F32)] * 2
    R = [cols // LANE >> level for level in range(LEVELS)]
    for level in range(LEVELS):
        t, r, count = rows[level] + 2 * PAD, R[level], 2 if level else 1
        scratch += [vm(r, t), vm(r, t), vm(r + 1, t), vm(r, t), vm(r, t)]
        scratch += [vm(max(r // 2, 1), t)] * 2 + [vm(count, r, t)] * 3
    copies = 14 + CYCLES * 8 + n0 // SUB
    scratch += [
        vm(2, R[2], SUB), vm(4, R[3], SUB), vm(CYCLES, 2, 2, R[1], SUB), vm(CYCLES, 2, 2, R[1], SUB),
        vm(CYCLES, 2, 2, R[2], SUB), vm(CYCLES, 4, 2, R[3], SUB), vm(2, R[0], SUB), vm(2, R[1], SUB),
        vm(2, R[1], SUB), pltpu.VMEM((n0, cols // 2), F32),
        pltpu.SemaphoreType.DMA((copies,)), pltpu.SemaphoreType.DMA((copies,)), pltpu.SemaphoreType.DMA((2,)),
    ]
    out = [jax.ShapeDtypeStruct((n0, cols), F32)] + [jax.ShapeDtypeStruct((n0, cols // 2), F32)] * 2
    corr, mean, var = pl.pallas_call(
        functools.partial(entry, grid_count, own, rows),
        out_shape=out,
        in_specs=[pl.BlockSpec(memory_space=pl.ANY)] * 2,
        out_specs=[pl.BlockSpec(memory_space=pltpu.VMEM)] * 3,
        scratch_shapes=scratch,
        compiler_params=pltpu.CompilerParams(
            collective_id=0, has_side_effects=True, vmem_limit_bytes=48 * 1024 * 1024),
    )(log_coef, source)
    return corr[None], mean, var


def solution(mesh):
    spec = P("samp", "grid", None)
    return jax.shard_map(
        functools.partial(local, mesh.shape["grid"]), mesh=mesh, in_specs=(spec, spec),
        out_specs=(spec, P("grid", "samp"), P("grid", "samp")), check_vma=False)
```

```python
import functools

import jax
import jax.numpy as jnp
from jax import lax
from jax.experimental import pallas as pl
from jax.experimental.pallas import tpu as pltpu
from jax.sharding import PartitionSpec as P

CYCLES = 2
LEVELS = 5
SUB = 8
LANE = 128
PAD = 8
HALO = (8, 4, 8, 16, 8)
ROLLED = (True, True, False, False, False)
BATCH = 16
F32 = jnp.float32


def harmonic(a, b):
    return 2.0 * a * b / (a + b)


def iota(axis):
    return lax.broadcasted_iota(jnp.int32, (SUB, LANE), axis)


def roll(x, shift, axis):
    return pltpu.roll(x, shift % x.shape[axis], axis)


def q_next(x):
    return jnp.where(iota(1) < 112, roll(x, -16, 1), roll(x, -17, 1))


def q_prev(x):
    return jnp.where(iota(1) >= 16, roll(x, 16, 1), roll(x, 17, 1))


def swap_bits(tiles, count):
    tiles = list(tiles)
    for k in range(count):
        w = 1 << k
        bit = (iota(1) // w) % 2 == 1
        for t in range(len(tiles)):
            if t & w == 0:
                a, b = tiles[t], tiles[t | w]
                tiles[t] = jnp.where(bit, roll(b, w, 1), a)
                tiles[t | w] = jnp.where(bit, b, roll(a, -w, 1))
    return tiles


def kernel(grid_count, own, rows, lc_hbm, src_hbm, corr, mean, var, rawc, raws, lev, rc2, rc3, sb1, rv1, rb2, rb3, rv0,
           sc1, rv1c, rcorr, send_sem, recv_sem, load_sem):
    me = lax.axis_index("grid")
    samp = lax.axis_index("samp")
    n0 = own[0]
    counter = [0]
    planes = [lev[level]["c"].shape[0] for level in range(LEVELS)]
    H = HALO
    h0 = H[0]

    def rd(i):
        return pl.ds(PAD + i, SUB)

    def put(stores):
        for ref, at, value in stores or ():
            ref[at] = value

    def groups(level, body, lo=0, hi=None):
        hi = rows[level] // SUB if hi is None else hi
        if ROLLED[level]:
            def step(g, carry):
                put(body(pl.multiple_of(g * SUB, SUB)))
                return carry
            lax.fori_loop(lo, hi, step, 0)
        else:
            held = []
            for g in range(lo, hi):
                held += body(g * SUB) or []
                if len(held) >= BATCH:
                    put(held)
                    held = []
            put(held)

    def to_grid(dist, src, dst):
        k = counter[0]
        counter[0] += 1
        target = me + dist
        copy = pltpu.make_async_remote_copy(
            src_ref=src, dst_ref=dst, send_sem=send_sem.at[k], recv_sem=recv_sem.at[k],
            device_id={"grid": target}, device_id_type=pl.DeviceIdType.MESH)
        sends = target >= 0 if dist < 0 else target < grid_count
        source = me - dist
        gets = source < grid_count if dist < 0 else source >= 0
        return copy, sends, gets

    def start(items):
        for copy, sends, gets in items:
            @pl.when(sends)
            def _():
                copy.start()

    def finish(items):
        for copy, sends, gets in items:
            @pl.when(sends)
            def _():
                copy.wait_send()

            @pl.when(gets)
            def _():
                copy.wait_recv()

    load_c = pltpu.make_async_copy(lc_hbm.at[0], rawc.at[pl.ds(h0, n0)], load_sem.at[0])
    load_s = pltpu.make_async_copy(src_hbm.at[0], raws.at[pl.ds(h0, n0)], load_sem.at[1])
    load_c.start()
    load_s.start()

    edge = 2
    @pl.when(jnp.logical_or(me < edge, me >= grid_count - edge))
    def _():
        @pl.when(me == 0)
        def _():
            rawc[pl.ds(0, h0)] = jnp.zeros((h0, rawc.shape[1]), F32)
            raws[pl.ds(0, h0)] = jnp.zeros((h0, rawc.shape[1]), F32)

        @pl.when(me == grid_count - 1)
        def _():
            rawc[pl.ds(h0 + n0, h0)] = jnp.zeros((h0, rawc.shape[1]), F32)
            raws[pl.ds(h0 + n0, h0)] = jnp.zeros((h0, rawc.shape[1]), F32)

        for ref in (rc2, rc3):
            for i in range(ref.shape[0]):
                ref[i] = jnp.ones(ref.shape[1:], F32)
        for ref in (rv1, rb2, rb3, rv0, rv1c):
            for i in range(ref.shape[0]):
                ref[i] = jnp.zeros(ref.shape[1:], F32)

    barrier = pltpu.get_barrier_semaphore()
    for dist in (-2, -1, 1, 2):
        inside = me + dist >= 0 if dist < 0 else me + dist < grid_count

        @pl.when(inside)
        def _():
            pl.semaphore_signal(barrier, inc=1, device_id={"grid": me + dist}, device_id_type=pl.DeviceIdType.MESH)
    pl.semaphore_signal(barrier, inc=1, device_id={"samp": 1 - samp}, device_id_type=pl.DeviceIdType.MESH)
    below = jnp.minimum(me, 2)
    above = jnp.minimum(grid_count - 1 - me, 2)
    pl.semaphore_wait(barrier, 1 + below + above)

    raw_items = []
    for hbm, raw in ((lc_hbm, rawc), (src_hbm, raws)):
        raw_items.append(to_grid(-1, hbm.at[0, pl.ds(0, h0)], raw.at[pl.ds(h0 + n0, h0)]))
        raw_items.append(to_grid(1, hbm.at[0, pl.ds(n0 - h0, h0)], raw.at[pl.ds(0, h0)]))
    start(raw_items)

    tiles = rawc.shape[1] // LANE
    lane_bits = tiles.bit_length() - 1

    def split(raw, out, fn, lo, hi):
        def step(g, carry):
            base = pl.multiple_of(g * SUB, SUB)
            y = swap_bits([raw[pl.ds(base, SUB), t * LANE:(t + 1) * LANE] for t in range(tiles)], lane_bits)
            for r in range(tiles):
                out[r, rd(base)] = fn(y[r])
            return carry
        lax.fori_loop(lo, hi, step, 0)

    def same(x):
        return x

    def children(level, j):
        return 2 * (j - H[level]) + H[level - 1]

    def gather_pairs(level, out, starts, scale=None):
        t = lev[level - 1]["t"]
        for k in range(planes[level]):
            for j in starts:
                first = PAD + children(level, j)
                x = t[k, pl.ds(first, SUB, stride=2)] + t[k, pl.ds(first + 1, SUB, stride=2)]
                out[k, rd(j)] = x if scale is None else scale * x

    def reduce_field(level, field, out, starts, lo, hi, scale=None):
        t = lev[level - 1]["t"]

        def body(i):
            return [(t, (k, rd(i)), field[2 * k, rd(i)] + field[2 * k + 1, rd(i)]) for k in range(planes[level])]
        groups(level - 1, body, lo, hi)
        gather_pairs(level, out, starts, scale)

    def own_starts(level):
        return range(H[level], H[level] + own[level], SUB)

    def all_starts(level):
        return range(0, rows[level], SUB)

    gh, gn = h0 // SUB, n0 // SUB
    c0, b0 = lev[0]["c"], lev[0]["b"].at[0]
    load_c.wait()
    split(rawc, c0, jnp.exp, gh, gh + gn)
    reduce_field(1, c0, lev[1]["c"], own_starts(1), gh, gh + gn, 0.25)
    reduce_field(2, lev[1]["c"], lev[2]["c"], own_starts(2), 0, None, 0.25)
    reduce_field(3, lev[2]["c"], lev[3]["c"], own_starts(3), 1, 3, 0.25)
    c2, c3 = lev[2]["c"], lev[3]["c"]

    def edges(ref, level):
        at = PAD + H[level]
        return pl.ds(at, SUB), pl.ds(at + own[level] - SUB, SUB)

    top2, bottom2 = edges(c2, 2)
    mine3 = pl.ds(PAD + H[3], own[3])
    coef_items = [
        to_grid(-1, c2.at[:, top2], rc2.at[1]),
        to_grid(1, c2.at[:, bottom2], rc2.at[0]),
        to_grid(-1, c3.at[:, mine3], rc3.at[2]),
        to_grid(-2, c3.at[:, mine3], rc3.at[3]),
        to_grid(1, c3.at[:, mine3], rc3.at[1]),
        to_grid(2, c3.at[:, mine3], rc3.at[0]),
    ]
    start(coef_items)
    load_s.wait()
    split(raws, b0, same, gh, gh + gn)
    finish(raw_items)
    for raw, out, fn in ((rawc, c0, jnp.exp), (raws, b0, same)):
        split(raw, out, fn, 0, gh)
        split(raw, out, fn, gh + gn, gh + gn + gh)
    reduce_field(1, c0, lev[1]["c"], all_starts(1), 0, None, 0.25)

    def weights(level):
        L = lev[level]
        R = planes[level]
        c = L["c"]
        first = H[level] - me * own[level]
        end = H[level] + (grid_count - me) * own[level]

        def vertical(i):
            at = iota(0) + i
            stores = []
            for r in range(R):
                a, b = c[r, rd(i - 1)], c[r, rd(i)]
                x = harmonic(jnp.where(at == first, b, a), jnp.where(at == end, a, b))
                stores.append((L["nf"], (r, rd(i)), x))
            return stores
        groups(level, vertical)

        def body(i):
            at = iota(0) + i
            inside = jnp.logical_and(at >= first, at < end)
            u = [c[r, rd(i)] for r in range(R)]
            we, ee = iota(1) == 0, iota(1) == LANE - 1
            faces = [harmonic(jnp.where(we, u[0], q_prev(u[-1])), u[0])]
            faces += [harmonic(u[r - 1], u[r]) for r in range(1, R)]
            faces += [harmonic(u[-1], jnp.where(ee, u[-1], q_next(u[0])))]
            for r in range(R):
                d = faces[r] + faces[r + 1] + L["nf"][r, rd(i)] + L["nf"][r, rd(i + 1)]
                L["d"][r, rd(i)] = d
                L["di"][r, rd(i)] = jnp.where(inside, 0.8 / d, 0.0)
            for r in range(R + 1):
                edge = we if r == 0 else ee
                L["hf"][r, rd(i)] = jnp.where(edge, 0.0, faces[r]) if r in (0, R) else faces[r]
        groups(level, body)

    def around(level, v, i, out):
        L = lev[level]
        R = planes[level]
        count = v.shape[0]
        prev, here, first, west = [], [], [], []
        for pr in range(count):
            first.append(v[pr, 0, rd(i)])
            west.append(q_prev(v[pr, R - 1, rd(i)]))
        here = list(first)
        for r in range(R):
            wf, ef = L["hf"][r, rd(i)], L["hf"][r + 1, rd(i)]
            nf, sf = L["nf"][r, rd(i)], L["nf"][r, rd(i + 1)]
            for pr in range(count):
                after = v[pr, r + 1, rd(i)] if r + 1 < R else None
                east = after if r + 1 < R else q_next(first[pr])
                total = (wf * west[pr] + ef * east) + (nf * v[pr, r, rd(i - 1)] + sf * v[pr, r, rd(i + 1)])
                out(pr, r, here[pr], total)
                west[pr], here[pr] = here[pr], after

    def sweep(level, src, dst, lo=0, hi=None):
        L = lev[level]

        def body(i):
            stores = []

            def out(pr, r, u, total):
                x = 0.2 * u + L["di"][r, rd(i)] * (L["b"][pr, r, rd(i)] + total)
                stores.append((dst, (pr, r, rd(i)), x))
            around(level, src, i, out)
            return stores
        groups(level, body, lo, hi)

    def first_sweep(level, dst):
        L = lev[level]

        def body(i):
            return [(dst, (pr, r, rd(i)), L["di"][r, rd(i)] * L["b"][pr, r, rd(i)])
                    for r in range(planes[level]) for pr in range(dst.shape[0])]
        groups(level, body)

    def restrict(level, v, starts):
        L = lev[level]
        t2 = (L["t"], L["t2"]) if level else (L["t"],)

        def body(i):
            held, stores = {}, []

            def out(pr, r, u, total):
                x = L["b"][pr, r, rd(i)] - L["d"][r, rd(i)] * u + total
                if r % 2 == 0:
                    held[pr] = x
                else:
                    stores.append((t2[pr], (r // 2, rd(i)), held[pr] + x))
            around(level, v, i, out)
            return stores
        groups(level, body)
        for pr in range(v.shape[0]):
            out = lev[level + 1]["b"]
            for k in range(planes[level + 1]):
                for j in starts:
                    first = PAD + children(level + 1, j)
                    out[pr, k, rd(j)] = (t2[pr][k, pl.ds(first, SUB, stride=2)]
                                         + t2[pr][k, pl.ds(first + 1, SUB, stride=2)])

    def correct(level, v, e, starts, pairs, sign=1.0):
        def body(k):
            stores = []
            for pr, pe in pairs:
                for j in starts:
                    x = e[pe, k, rd(j)]
                    first = PAD + children(level + 1, j)
                    for r in range(2):
                        for h in range(2):
                            at = pl.ds(first + h, SUB, stride=2)
                            y = v[pr, 2 * k + r, at]
                            stores.append((v, (pr, 2 * k + r, at), y + x if sign > 0 else y - x))
            put(stores)
        if ROLLED[level]:
            lax.fori_loop(0, planes[level + 1], lambda k, c: (body(k), c)[1], 0)
        else:
            for k in range(planes[level + 1]):
                body(k)

    weights(0)
    weights(1)
    b1, v1a, v1b = lev[1]["b"], lev[1]["va"], lev[1]["vb"]
    v0a, v0b = lev[0]["va"], lev[0]["vb"]
    reduce_field(1, b0, b1.at[1], all_starts(1), 0, None)
    h1, n1 = H[1], own[1]
    R1 = planes[1]
    both = ((0, 0), (1, 1))

    for cycle in range(CYCLES):
        if cycle == 0:
            first_sweep(0, v0b)
        else:
            sweep(0, v0a, v0b, 0, gh + 1)
            sweep(0, v0a, v0b, gh + gn - 1, None)
        sweep(0, v0b, v0a)
        restrict(0, v0a, all_starts(1))
        if cycle == 0:
            first_sweep(1, v1b)
        else:
            def clear(i):
                for r in range(R1):
                    v1a[0, r, rd(i)] = jnp.zeros((SUB, LANE), F32)
            groups(1, clear)
            sweep(1, v1a, v1b)
        sweep(1, v1b, v1a)
        restrict(1, v1a, own_starts(2))
        b2 = lev[2]["b"]
        for pr in range(2):
            for r in range(R1):
                sb1[cycle, 0, pr, r] = v1a[pr, r, rd(h1)]
                sb1[cycle, 1, pr, r] = v1a[pr, r, rd(h1 + n1 - SUB)]
        items = [
            to_grid(-1, b2.at[:, :, top2], rb2.at[cycle, 1]),
            to_grid(1, b2.at[:, :, bottom2], rb2.at[cycle, 0]),
            to_grid(-1, sb1.at[cycle, 0], rv1.at[cycle, 1]),
            to_grid(1, sb1.at[cycle, 1], rv1.at[cycle, 0]),
        ]
        start(items)
        if cycle == 0:
            finish(coef_items)
            for r in range(planes[2]):
                c2[r, rd(0)] = rc2[0, r]
                c2[r, rd(H[2] + own[2])] = rc2[1, r]
            for s, at in enumerate((0, SUB, H[3] + SUB, H[3] + 2 * SUB)):
                for r in range(planes[3]):
                    c3[r, rd(at)] = rc3[s, r]
            reduce_field(4, c3, lev[4]["c"], all_starts(4), 0, None, 0.25)
            for level in (2, 3, 4):
                weights(level)
        finish(items)
        for pr in range(2):
            for r in range(planes[2]):
                b2[pr, r, rd(0)] = rb2[cycle, 0, pr, r]
                b2[pr, r, rd(H[2] + own[2])] = rb2[cycle, 1, pr, r]
            for r in range(R1):
                v1a[pr, r, pl.ds(PAD, h1)] = rv1[cycle, 0, pr, r, SUB - h1:, :]
                v1a[pr, r, pl.ds(PAD + h1 + n1, h1)] = rv1[cycle, 1, pr, r, :h1, :]
        v2a, v2b = lev[2]["va"], lev[2]["vb"]
        first_sweep(2, v2b)
        sweep(2, v2b, v2a)
        restrict(2, v2a, own_starts(3))
        b3 = lev[3]["b"]
        mine = b3.at[:, :, mine3]
        items = [
            to_grid(-1, mine, rb3.at[cycle, 2]),
            to_grid(-2, mine, rb3.at[cycle, 3]),
            to_grid(1, mine, rb3.at[cycle, 1]),
            to_grid(2, mine, rb3.at[cycle, 0]),
        ]
        start(items)
        finish(items)
        for s, at in enumerate((0, SUB, H[3] + SUB, H[3] + 2 * SUB)):
            for pr in range(2):
                for r in range(planes[3]):
                    b3[pr, r, rd(at)] = rb3[cycle, s, pr, r]
        v3a, v3b = lev[3]["va"], lev[3]["vb"]
        v4a, v4b = lev[4]["va"], lev[4]["vb"]
        first_sweep(3, v3b)
        sweep(3, v3b, v3a)
        restrict(3, v3a, all_starts(4))
        first_sweep(4, v4b)
        sweep(4, v4b, v4a)
        sweep(4, v4a, v4b)
        sweep(4, v4b, v4a)
        correct(3, v3a, v4a, all_starts(4), both)
        sweep(3, v3a, v3b)
        sweep(3, v3b, v3a)
        correct(2, v2a, v3a, (H[3] - 4, H[3] + 4), both)
        sweep(2, v2a, v2b)
        sweep(2, v2b, v2a)
        correct(1, v1a, v2a, (H[2] - 2, H[2] + 6, H[2] + 14), both)
        sweep(1, v1a, v1b)
        sweep(1, v1b, v1a)
        correct(0, v0a, v1a, all_starts(1), ((0, 0),))
        sweep(0, v0a, v0b)
        if cycle == CYCLES - 1:
            sweep(0, v0b, v0a, gh, gh + gn)
        else:
            sweep(0, v0b, v0a, gh, gh + 1)
            sweep(0, v0b, v0a, gh + gn - 1, gh + gn)
            for r in range(R1):
                sc1[0, r] = v1a[1, r, rd(h1)]
                sc1[1, r] = v1a[1, r, rd(h1 + n1 - SUB)]
            top0, bottom0 = edges(v0a, 0)
            items = [
                to_grid(-1, v0a.at[0, :, top0], rv0.at[1]),
                to_grid(1, v0a.at[0, :, bottom0], rv0.at[0]),
                to_grid(-1, sc1.at[0], rv1c.at[1]),
                to_grid(1, sc1.at[1], rv1c.at[0]),
            ]
            start(items)
            sweep(0, v0b, v0a, gh + 1, gh + gn - 1)
            sweep(0, v0a, v0b, gh + 1, gh + gn - 1)
            finish(items)
            for r in range(planes[0]):
                v0a[0, r, rd(0)] = rv0[0, r]
                v0a[0, r, rd(h0 + n0)] = rv0[1, r]
            for r in range(R1):
                v1a[1, r, pl.ds(PAD, h1)] = rv1c[0, r, SUB - h1:, :]
                v1a[1, r, pl.ds(PAD + h1 + n1, h1)] = rv1c[1, r, :h1, :]
    correct(0, v0a, v1a, own_starts(1), ((0, 1),), -1.0)

    half = corr.shape[1] // 2
    first = counter[0]

    def corr_copy(g):
        base = pl.multiple_of(g * SUB, SUB)
        there = pl.multiple_of((1 - samp) * half, LANE)
        return pltpu.make_async_remote_copy(
            src_ref=corr.at[pl.ds(base, SUB), pl.ds(there, half)], dst_ref=rcorr.at[pl.ds(base, SUB)],
            send_sem=send_sem.at[first + g], recv_sem=recv_sem.at[first + g],
            device_id={"samp": 1 - samp}, device_id_type=pl.DeviceIdType.MESH)

    def emit(g, carry):
        base = pl.multiple_of(g * SUB, SUB)
        y = swap_bits([v0a[0, r, rd(h0 + base)] for r in range(tiles)], lane_bits)
        for t in range(tiles):
            corr[pl.ds(base, SUB), t * LANE:(t + 1) * LANE] = y[t]
        corr_copy(g).start()
        return carry
    lax.fori_loop(0, gn, emit, 0)

    def combine(g, carry):
        base = pl.multiple_of(g * SUB, SUB)
        corr_copy(g).wait()
        here = pl.multiple_of(samp * half, LANE)
        a = corr[pl.ds(base, SUB), pl.ds(here, half)]
        b = rcorr[pl.ds(base, SUB)]
        m = (a + b) / 2.0
        mean[pl.ds(base, SUB)] = m
        var[pl.ds(base, SUB)] = a * a + b * b - 2.0 * m * m
        return carry
    lax.fori_loop(0, gn, combine, 0)


NAMES = ("c", "nf", "hf", "d", "di", "t", "t2", "b", "va", "vb")


def entry(grid_count, own, rows, *refs):
    refs = list(refs)
    head, rest = refs[:7], refs[7:]
    lev = {}
    for level in range(LEVELS):
        lev[level] = dict(zip(NAMES, rest[:len(NAMES)]))
        rest = rest[len(NAMES):]
    kernel(grid_count, own, rows, *head, lev, *rest)


def local(grid_count, log_coef, source):
    _, n0, cols = log_coef.shape
    own = tuple(n0 >> level for level in range(LEVELS))
    rows = tuple(-(-(own[level] + 2 * HALO[level]) // SUB) * SUB for level in range(LEVELS))
    assert cols == LANE << (LEVELS - 1) and own[LEVELS - 1] * 2 == SUB

    def vm(*shape):
        return pltpu.VMEM(shape + (LANE,), F32)

    scratch = [pltpu.VMEM((n0 + 2 * HALO[0], cols), F32)] * 2
    R = [cols // LANE >> level for level in range(LEVELS)]
    for level in range(LEVELS):
        t, r, count = rows[level] + 2 * PAD, R[level], 2 if level else 1
        t += SUB * (1 - t // SUB % 2)
        scratch += [vm(r, t), vm(r, t), vm(r + 1, t), vm(r, t), vm(r, t)]
        scratch += [vm(max(r // 2, 1), t)] * 2 + [vm(count, r, t)] * 3
    copies = 14 + CYCLES * 8 + n0 // SUB
    scratch += [
        vm(2, R[2], SUB), vm(4, R[3], SUB), vm(CYCLES, 2, 2, R[1], SUB), vm(CYCLES, 2, 2, R[1], SUB),
        vm(CYCLES, 2, 2, R[2], SUB), vm(CYCLES, 4, 2, R[3], SUB), vm(2, R[0], SUB), vm(2, R[1], SUB),
        vm(2, R[1], SUB), pltpu.VMEM((n0, cols // 2), F32),
        pltpu.SemaphoreType.DMA((copies,)), pltpu.SemaphoreType.DMA((copies,)), pltpu.SemaphoreType.DMA((2,)),
    ]
    out = [jax.ShapeDtypeStruct((n0, cols), F32)] + [jax.ShapeDtypeStruct((n0, cols // 2), F32)] * 2
    corr, mean, var = pl.pallas_call(
        functools.partial(entry, grid_count, own, rows),
        out_shape=out,
        in_specs=[pl.BlockSpec(memory_space=pl.ANY)] * 2,
        out_specs=[pl.BlockSpec(memory_space=pltpu.VMEM)] * 3,
        scratch_shapes=scratch,
        compiler_params=pltpu.CompilerParams(
            collective_id=0, has_side_effects=True, vmem_limit_bytes=48 * 1024 * 1024),
    )(log_coef, source)
    return corr[None], mean, var


def solution(mesh):
    spec = P("samp", "grid", None)
    return jax.shard_map(
        functools.partial(local, mesh.shape["grid"]), mesh=mesh, in_specs=(spec, spec),
        out_specs=(spec, P("grid", "samp"), P("grid", "samp")), check_vma=False)
```
